512 devices in a mesh: pts: 64 (over x, y, core), blk: 8 (over z).
Axes of the slice: x: 4, y: 8, z: 8, core: 2. Of those that a mesh axis runs over, the one named last changes fastest.
Arguments:
- deviations: bfloat16 [3145728, 256], P(('pts', 'blk')), may hold values from -24 to 24
- basis: bfloat16 [3145728, 64], P(('pts', 'blk')), may hold values from -0.0034179688 to 0.0034179688
- sensitivity: bfloat16 [64, 512, 512], P('pts', 'blk'), may hold values from -0.75 to 0.75
- blade_ids: int32 [24], replicated, may hold values from 0 to 255, as said below
Outputs:
- gram: float32 [256, 256], P('pts', 'blk')
- change: float32 [24, 512, 512], P(None, 'blk', 'pts')
The draws below stay inside these ranges and needn't reach their ends.
Inputs may be any that keep to these rules, and one draw needn't show every extreme that they name: `blade_ids`: distinct blade numbers; blade 0 and blade 256 - 1 are always among them.
All inputs are finite; a program needn't handle non-finite values.
Results may differ from the reference program's by a relative error of at most 0.0003.
Values may be sent and summed in bfloat16 or wider, within the bound.
No kernel may reach another device: no remote copies, remote signals or barrier semaphores. Data moves between devices by JAX's collectives and lax.ppermute only.
A program may use at most 64 MiB of HBM per device.

```python
import jax
import jax.numpy as jnp
from jax import lax

NBLADE = 256
NSHAPE = 64
ORDER = 512
NREAL = 24
ROWS = 6144
NPTS = 3145728


def draw_blade_ids(key, part):
    first_key, second_key = jax.random.split(key)
    inner = jax.random.permutation(first_key, NBLADE - 2)[:NREAL - 2] + 1
    chosen = jnp.concatenate([inner.astype(jnp.int32), jnp.array([0, NBLADE - 1], jnp.int32)])
    return jax.random.permutation(second_key, chosen).astype(jnp.int32)


def spiked(values, own_key, source, target, blocks, factor):
    def block_of(axis_at):
        return (jnp.arange(values.shape[axis_at]) // (values.shape[axis_at] // blocks)).reshape((-1,) + (1,) * (values.ndim - 1 - axis_at))

    near = jax.random.permutation(own_key, blocks)[block_of(target)]
    far = (block_of(target) + blocks // 2) % blocks
    return jnp.where((block_of(source) == near) | (block_of(source) == far), factor * values, values)


def level_of(own_key, shape, shards, least, largest):
    def one(dim, parts):
        heights = jax.random.uniform(jax.random.fold_in(jax.random.fold_in(own_key, 6), dim), (parts,), jnp.float32, least / len(shards), largest / len(shards))
        return jnp.repeat(jnp.exp(heights), shape[dim] // parts).reshape((-1,) + (1,) * (len(shape) - dim - 1))

    gain = one(*shards[0])
    for cut in shards[1:]:
        gain = gain * one(*cut)
    return gain


def noise(key, shape, scale, bound, cuts=(), held_as=jnp.bfloat16):
    result = jax.random.normal(key, shape, jnp.float32) * scale
    if len(cuts) > 0:
        result = level_of(key, shape, cuts, -0.22, 0.18) * result
    return jnp.clip(result, min=-bound, max=bound).astype(held_as)


def bell_draw_with(stream_key, shape, width, most, shards, heavy, held_as=jnp.bfloat16):
    values = width * jax.random.normal(stream_key, shape, jnp.float32)
    if shards:
        values = values * level_of(stream_key, shape, shards, -0.22, 0.18)
    return jnp.clip(spiked(values, jax.random.fold_in(stream_key, 3), *heavy), -most, most).astype(held_as)


def setup_inputs(seed: int = 0) -> dict:
    key_list = jax.random.split(jax.random.key(seed), 5)
    deviations = bell_draw_with(key_list[0], (NPTS, NBLADE), 1.0, 24.0, ((0, 512),), (0, 1, 256, 6.0))
    basis = noise(key_list[1], (NPTS, NSHAPE), NPTS ** -0.5, 0.0034179688, ((0, 512),))
    sensitivity = noise(key_list[2], (NSHAPE, ORDER, ORDER), NSHAPE ** -0.5, 0.75, ((0, 64), (1, 8)))
    blade_ids = draw_blade_ids(jax.random.fold_in(key_list[4], 71), 0)
    return {"deviations": deviations, "basis": basis, "sensitivity": sensitivity, "blade_ids": blade_ids}


def reference(deviations, basis, sensitivity, blade_ids):
    count = NPTS // ROWS

    def accumulate(index, carry):
        gram_sum, coeff_sum, energy_sum = carry
        start = (index * ROWS).astype(jnp.int32)
        block = lax.dynamic_slice_in_dim(deviations, start, ROWS, 0)
        shapes = lax.dynamic_slice_in_dim(basis, start, ROWS, 0)
        dims = (((0,), (0,)), ((), ()))
        gram_sum = gram_sum + lax.dot_general(block, block, dims, preferred_element_type=jnp.float32)
        coeff_sum = coeff_sum + lax.dot_general(shapes, block, dims, preferred_element_type=jnp.float32)
        wide = block.astype(jnp.float32)
        energy_sum = energy_sum + lax.optimization_barrier(jnp.sum(wide * wide, axis=0))
        return (gram_sum, coeff_sum, energy_sum)
    init = (jnp.zeros((NBLADE, NBLADE), jnp.float32), jnp.zeros((NSHAPE, NBLADE), jnp.float32), jnp.zeros((NBLADE,), jnp.float32))
    gram_sum, coeffs, energy_sum = lax.fori_loop(0, count, accumulate, init)
    gram = gram_sum / NPTS
    energy = energy_sum / NPTS
    weights = coeffs[:, blade_ids] / jnp.sqrt(energy[blade_ids] + 1e-05)
    change = jnp.einsum('kb,kij->bij', weights, sensitivity.astype(jnp.float32), precision=lax.Precision.HIGHEST)
    return (gram, change)
```

```python
import functools

import jax
import jax.numpy as jnp
from jax import lax
from jax.experimental import pallas as pl
from jax.experimental.pallas import tpu as pltpu
from jax.sharding import Mesh, PartitionSpec as P

F32 = jnp.float32
HIGHEST = lax.Precision.HIGHEST
VMEM = pl.BlockSpec(memory_space=pltpu.VMEM)
SMEM = pl.BlockSpec(memory_space=pltpu.SMEM)

NX, NY, NC, NZ = 4, 8, 2, 8
BLADES, SHAPES, ORDER, REAL = 256, 64, 512, 24
CHUNKS = 4


def params(mib):
    return pltpu.CompilerParams(vmem_limit_bytes=mib * 1024 * 1024)


def halves(first, second):
    axis = first.ndim - 2
    row = lax.broadcasted_iota(jnp.int32, first.shape, axis)
    upper = jnp.where(row < 4, first, pltpu.roll(second, 4, axis))
    lower = jnp.where(row < 4, pltpu.roll(first, 4, axis), second)
    return upper, lower


def products_kernel(ids_ref, dev_ref, basis_ref, sens_ref, out_ref, gram_ref, coef_ref, turned_ref):
    step = pl.program_id(0)
    dev = dev_ref[...]
    gram = lax.dot_general(dev, dev, (((0,), (0,)), ((), ())), preferred_element_type=F32)
    coef = jnp.dot(basis_ref[...], dev, preferred_element_type=F32)

    @pl.when(step == 0)
    def _():
        gram_ref[...] = gram
        coef_ref[...] = coef
        turned_ref[...] = sens_ref[...].astype(F32).T
        even = turned_ref[pl.ds(0, ORDER // 2, 2), :]
        odd = turned_ref[pl.ds(1, ORDER // 2, 2), :]
        rows = jnp.concatenate([even, odd], axis=1).reshape(16, 2, 8, 128)
        parts = halves(rows[:, 0], rows[:, 1])
        for x in range(NX):
            for c in range(NC):
                out_ref[2 * x + c, 64:96] = parts[c][4 * x : 4 * x + 4].reshape(32, 128)

    @pl.when(step > 0)
    def _():
        gram_ref[...] += gram
        coef_ref[...] += coef

    @pl.when(step == CHUNKS - 1)
    def _():
        total = gram_ref[...]
        parts = halves(total[:, :128].reshape(32, 8, 128), total[:, 128:].reshape(32, 8, 128))
        for x in range(NX):
            for c in range(NC):
                out_ref[2 * x + c, 0:64] = parts[c][8 * x : 8 * x + 8].reshape(64, 128)
        row = lax.broadcasted_iota(jnp.int32, (BLADES, BLADES), 0)
        col = lax.broadcasted_iota(jnp.int32, (BLADES, BLADES), 1)
        energy = jnp.sum(jnp.where(row == col, total, 0.0), axis=0, keepdims=True)
        table = jnp.concatenate([coef_ref[...], jnp.broadcast_to(energy, (8, BLADES))], axis=0)
        real = lax.broadcasted_iota(jnp.int32, (REAL, BLADES), 0)
        blade = lax.broadcasted_iota(jnp.int32, (REAL, BLADES), 1)
        wanted = jnp.zeros((REAL, BLADES), jnp.int32)
        for r in range(REAL):
            wanted = jnp.where(real == r, ids_ref[r], wanted)
        chosen = (blade == wanted).astype(F32)
        picked = lax.dot_general(
            chosen, table, (((1,), (1,)), ((), ())), precision=HIGHEST, preferred_element_type=F32
        )
        old = lax.broadcasted_iota(jnp.int32, (SHAPES + 8, 128), 0)
        new = lax.broadcasted_iota(jnp.int32, (SHAPES + 8, 128), 1)
        place = jnp.where(old < SHAPES, 8 * ((old // 2) % NY) + 2 * (old // 16) + old % 2, old)
        order = ((place == new) & (old <= SHAPES)).astype(F32)
        picked = jnp.dot(picked, order, precision=HIGHEST, preferred_element_type=F32)
        first, second, third = picked[0:8], picked[8:16], picked[16:24]
        lane = lax.broadcasted_iota(jnp.int32, (8, 128), 1)
        upper = jnp.where(lane < 64, first, pltpu.roll(third, 64, 1))
        lower = jnp.where(lane < 64, second, 0.0)
        lower = jnp.where(lane == 64, first, lower)
        lower = jnp.where(lane == 65, pltpu.roll(second, 1, 1), lower)
        lower = jnp.where(lane == 66, pltpu.roll(third, 2, 1), lower)
        for s in range(NX * NC):
            out_ref[s, 96:104] = upper
            out_ref[s, 104:112] = lower


def products(ids, dev, basis, sens):
    rows = dev.shape[0] // CHUNKS
    return pl.pallas_call(
        products_kernel,
        grid=(CHUNKS,),
        in_specs=[
            SMEM,
            pl.BlockSpec((rows, BLADES), lambda i: (i, 0)),
            pl.BlockSpec((SHAPES, rows), lambda i: (0, i)),
            pl.BlockSpec((SHAPES, ORDER), lambda i: (0, 0)),
        ],
        out_specs=pl.BlockSpec((NX * NC, 112, 128), lambda i: (0, 0, 0)),
        out_shape=jax.ShapeDtypeStruct((NX * NC, 112, 128), F32),
        scratch_shapes=[
            pltpu.VMEM((BLADES, BLADES), F32),
            pltpu.VMEM((SHAPES, BLADES), F32),
            pltpu.VMEM((ORDER, SHAPES), F32),
        ],
        compiler_params=params(32),
        name="products",
    )(ids, dev, basis, sens)


def after_xc_kernel(in_ref, out_ref):
    gram = in_ref[0, 0:64]
    coef = in_ref[0, 96:112]
    for s in range(1, NX * NC):
        gram += in_ref[s, 0:64]
        coef += in_ref[s, 96:112]
    for y in range(NY):
        out_ref[y, 0:8] = gram[8 * y : 8 * y + 8]
        out_ref[y, 8:24] = coef
    for a in range(NX):
        first = in_ref[2 * a, 64:96].reshape(4, 8, 128)
        second = in_ref[2 * a + 1, 64:96].reshape(4, 8, 128)
        parts = halves(first, second)
        for y in range(NY):
            out_ref[y, 24 + 8 * a : 32 + 8 * a] = parts[y % 2][y // 2]


def after_y_kernel(in_ref, out_ref):
    gram = in_ref[0, 0:8]
    coef = in_ref[0, 8:24]
    for y in range(1, NY):
        gram += in_ref[y, 0:8]
        coef += in_ref[y, 8:24]
    row = lax.broadcasted_iota(jnp.int32, (8, 128), 0)
    lane = lax.broadcasted_iota(jnp.int32, (8, 128), 1)
    turned = pltpu.roll(gram, 4, 0)
    for z in range(NZ):
        block = gram if z < 4 else turned
        if z % 4 != 3:
            block = pltpu.roll(block, 96 - 32 * (z % 4), 1)
        out_ref[z, 0:8] = coef[0:8]
        out_ref[z, 8:16] = jnp.where((row < 4) & (lane >= 96), block, coef[8:16])


def final_kernel(points, in_ref, sens_ref, gram_ref, change_ref):
    total = in_ref[0]
    for z in range(1, NZ):
        total += in_ref[z]
    upper, lower = total[0:8], total[8:16]
    gram_ref[...] = pltpu.roll(lower, 32, 1)[0:4, 0:32] / points
    coef = (upper, lower, pltpu.roll(upper, 64, 1))
    weights = []
    for a in range(3):
        energy = lower[:, 64 + a : 65 + a] / points
        weights.append(coef[a][:, 0:SHAPES] / jnp.sqrt(energy + 1e-05))
    weights = jnp.concatenate(weights, axis=0)
    for q in range(4):
        rows = [sens_ref[y, pl.ds(24 + q, 8, 4), :] for y in range(NY)]
        block = jnp.dot(
            weights, jnp.concatenate(rows, axis=0), precision=HIGHEST, preferred_element_type=F32
        )
        change_ref[pl.ds(2 * q, REAL, 8), :] = block[:, 0:64]
        change_ref[pl.ds(2 * q + 1, REAL, 8), :] = block[:, 64:128]


def call(kernel, shape, count, name):
    return pl.pallas_call(
        kernel,
        in_specs=[VMEM] * count,
        out_specs=jax.tree.map(lambda _: VMEM, shape),
        out_shape=shape,
        compiler_params=params(8),
        name=name,
    )


def on_device(deviations, basis, sensitivity, blade_ids):
    points = float(deviations.shape[0] * NX * NY * NC * NZ)
    exchange = functools.partial(lax.all_to_all, split_axis=0, concat_axis=0, tiled=True)
    part = products(blade_ids, deviations, basis.T, sensitivity[0])
    part = exchange(part, ("x", "c"))
    part = call(after_xc_kernel, jax.ShapeDtypeStruct((NY, 56, 128), F32), 1, "after_xc")(part)
    by_y = exchange(part, "y")
    part = call(after_y_kernel, jax.ShapeDtypeStruct((NZ, 16, 128), F32), 1, "after_y")(by_y)
    by_z = exchange(part, "z")
    gram, change = call(
        functools.partial(final_kernel, points),
        (
            jax.ShapeDtypeStruct((4, 32), F32),
            jax.ShapeDtypeStruct((REAL * 8, 64), F32),
        ),
        2,
        "final",
    )(by_z, by_y)
    return gram, change.reshape(REAL, 8, 64).transpose(0, 2, 1)


def solution(mesh):
    fine = Mesh(mesh.devices.reshape(NX, NY, NC, NZ), ("x", "y", "c", "z"))
    pts = ("x", "y", "c")
    rows = P((*pts, "z"), None)
    return jax.shard_map(
        on_device,
        mesh=fine,
        in_specs=(rows, rows, P(pts, "z", None), P()),
        out_specs=(P(pts, "z"), P(None, "z", pts)),
        check_vma=False,
    )
```

```python
import functools

import jax
import jax.numpy as jnp
from jax import lax
from jax.experimental import pallas as pl
from jax.experimental.pallas import tpu as pltpu
from jax.sharding import Mesh, PartitionSpec as P

F32 = jnp.float32
HIGHEST = lax.Precision.HIGHEST
VMEM = pl.BlockSpec(memory_space=pltpu.VMEM)

NX, NY, NC, NZ = 4, 8, 2, 8
BLADES, SHAPES, ORDER, REAL = 256, 64, 512, 24
CHUNKS = 4


def params(mib):
    return pltpu.CompilerParams(vmem_limit_bytes=mib * 1024 * 1024)


def halves(first, second):
    axis = first.ndim - 2
    row = lax.broadcasted_iota(jnp.int32, first.shape, axis)
    upper = jnp.where(row < 4, first, pltpu.roll(second, 4, axis))
    lower = jnp.where(row < 4, pltpu.roll(first, 4, axis), second)
    return upper, lower


def products_kernel(ids_hbm, dev_hbm, basis_hbm, sens_hbm, out_ref, ids_ref, dev_ref, basis_ref, sens_ref, gram_ref, turned_ref, picked_ref, sems):
    rows = dev_ref.shape[0] // CHUNKS
    sens_copy = pltpu.make_async_copy(sens_hbm, sens_ref, sems.at[2 * CHUNKS])
    ids_copy = pltpu.make_async_copy(ids_hbm, ids_ref, sems.at[2 * CHUNKS + 1])
    copies = []
    for i in range(CHUNKS):
        span = pl.ds(i * rows, rows)
        copies.append(pltpu.make_async_copy(dev_hbm.at[span, :], dev_ref.at[span, :], sems.at[2 * i]))
        copies.append(
            pltpu.make_async_copy(basis_hbm.at[:, span], basis_ref.at[:, span], sems.at[2 * i + 1])
        )
    sens_copy.start()
    for copy in copies:
        copy.start()
    ids_copy.start()

    sens_copy.wait()
    turned_ref[0:ORDER, :] = sens_ref[...].astype(F32).T
    even = turned_ref[pl.ds(0, ORDER // 2, 2), :]
    odd = turned_ref[pl.ds(1, ORDER // 2, 2), :]
    tiles = jnp.concatenate([even, odd], axis=1).reshape(16, 2, 8, 128)
    parts = halves(tiles[:, 0], tiles[:, 1])
    for x in range(NX):
        for c in range(NC):
            out_ref[2 * x + c, 64:96] = parts[c][4 * x : 4 * x + 4].reshape(32, 128)

    gram = coef = None
    for i in range(CHUNKS):
        copies[2 * i].wait()
        copies[2 * i + 1].wait()
        dev = dev_ref[i * rows : (i + 1) * rows, :]
        more = lax.dot_general(dev, dev, (((0,), (0,)), ((), ())), preferred_element_type=F32)
        gram = more if gram is None else gram + more
        more = jnp.dot(basis_ref[:, i * rows : (i + 1) * rows], dev, preferred_element_type=F32)
        coef = more if coef is None else coef + more
    gram_ref[...] = gram
    turned_ref[0:BLADES, :] = coef.T
    ids_copy.wait()

    parts = halves(gram[:, :128].reshape(32, 8, 128), gram[:, 128:].reshape(32, 8, 128))
    for x in range(NX):
        for c in range(NC):
            out_ref[2 * x + c, 0:64] = parts[c][8 * x : 8 * x + 8].reshape(64, 128)

    lane = lax.broadcasted_iota(jnp.int32, (1, BLADES), 1)
    for r in range(REAL):
        blade = ids_ref[r]
        picked_ref[r : r + 1, 0:SHAPES] = turned_ref[pl.ds(blade, 1), :]
        row = jnp.where(lane == blade, gram_ref[pl.ds(blade, 1), :], 0.0)
        picked_ref[r : r + 1, 128:256] = row[:, :128] + row[:, 128:]
    coef = [picked_ref[8 * a : 8 * a + 8, 0:128] for a in range(3)]
    energy = [jnp.sum(picked_ref[8 * a : 8 * a + 8, 128:256], axis=1, keepdims=True) for a in range(3)]
    lane = lax.broadcasted_iota(jnp.int32, (8, 128), 1)
    upper = jnp.where(lane < 64, coef[0], pltpu.roll(coef[2], 64, 1))
    lower = jnp.where(lane < 64, coef[1], 0.0)
    for a in range(3):
        lower = jnp.where(lane == 64 + a, energy[a], lower)
    for s in range(NX * NC):
        out_ref[s, 96:104] = upper
        out_ref[s, 104:112] = lower


def products(ids, dev, basis, sens):
    hbm = pl.BlockSpec(memory_space=pltpu.HBM)
    return pl.pallas_call(
        products_kernel,
        in_specs=[hbm] * 4,
        out_specs=VMEM,
        out_shape=jax.ShapeDtypeStruct((NX * NC, 112, 128), F32),
        scratch_shapes=[
            pltpu.SMEM((REAL,), jnp.int32),
            pltpu.VMEM(dev.shape, dev.dtype),
            pltpu.VMEM(basis.shape, basis.dtype),
            pltpu.VMEM(sens.shape, sens.dtype),
            pltpu.VMEM((BLADES, BLADES), F32),
            pltpu.VMEM((ORDER, SHAPES), F32),
            pltpu.VMEM((REAL, 256), F32),
            pltpu.SemaphoreType.DMA((2 * CHUNKS + 2,)),
        ],
        compiler_params=params(24),
        name="products",
    )(*(pltpu.with_memory_space_constraint(v, pltpu.HBM) for v in (ids, dev, basis, sens)))


def after_xc_kernel(in_ref, out_ref):
    gram = in_ref[0, 0:64]
    coef = in_ref[0, 96:112]
    for s in range(1, NX * NC):
        gram += in_ref[s, 0:64]
        coef += in_ref[s, 96:112]
    for y in range(NY):
        out_ref[y, 0:8] = gram[8 * y : 8 * y + 8]
        out_ref[y, 8:24] = coef
    for a in range(NX):
        first = in_ref[2 * a, 64:96].reshape(4, 8, 128)
        second = in_ref[2 * a + 1, 64:96].reshape(4, 8, 128)
        parts = halves(first, second)
        for y in range(NY):
            out_ref[y, 24 + 8 * a : 32 + 8 * a] = parts[y % 2][y // 2]


def after_y_kernel(in_ref, out_ref):
    gram = in_ref[0, 0:8]
    coef = in_ref[0, 8:24]
    for y in range(1, NY):
        gram += in_ref[y, 0:8]
        coef += in_ref[y, 8:24]
    row = lax.broadcasted_iota(jnp.int32, (8, 128), 0)
    lane = lax.broadcasted_iota(jnp.int32, (8, 128), 1)
    turned = pltpu.roll(gram, 4, 0)
    for z in range(NZ):
        block = gram if z < 4 else turned
        if z % 4 != 3:
            block = pltpu.roll(block, 96 - 32 * (z % 4), 1)
        out_ref[z, 0:8] = coef[0:8]
        out_ref[z, 8:16] = jnp.where((row < 4) & (lane >= 96), block, coef[8:16])


def final_kernel(points, in_ref, sens_ref, gram_ref, change_ref, block_ref):
    total = in_ref[0]
    for z in range(1, NZ):
        total += in_ref[z]
    upper, lower = total[0:8], total[8:16]
    gram_ref[...] = pltpu.roll(lower, 32, 1)[0:4, 0:32] / points
    coef = (upper, lower, pltpu.roll(upper, 64, 1))
    weights = []
    for a in range(3):
        energy = lower[:, 64 + a : 65 + a] / points
        weights.append(coef[a][:, 0:SHAPES] / jnp.sqrt(energy + 1e-05))
    weights = jnp.concatenate(weights, axis=0)
    for q in range(4):
        for x in range(NX):
            for c in range(NC):
                block_ref[pl.ds(16 * x + c, NY, 2), :] = sens_ref[
                    pl.ds(24 + 4 * (2 * x + c) + q, NY, 56), :
                ]
        block = jnp.dot(weights, block_ref[...], precision=HIGHEST, preferred_element_type=F32)
        change_ref[pl.ds(2 * q, REAL, 8), :] = block[:, 0:64]
        change_ref[pl.ds(2 * q + 1, REAL, 8), :] = block[:, 64:128]


def call(kernel, shape, count, name, scratch=()):
    return pl.pallas_call(
        kernel,
        in_specs=[VMEM] * count,
        out_specs=jax.tree.map(lambda _: VMEM, shape),
        out_shape=shape,
        scratch_shapes=scratch,
        compiler_params=params(8),
        name=name,
    )


def on_device(deviations, basis, sensitivity, blade_ids):
    points = float(deviations.shape[0] * NX * NY * NC * NZ)
    exchange = functools.partial(lax.all_to_all, split_axis=0, concat_axis=0, tiled=True)
    part = products(blade_ids, deviations, basis.T, sensitivity[0])
    part = exchange(part, ("x", "c"))
    part = call(after_xc_kernel, jax.ShapeDtypeStruct((NY, 56, 128), F32), 1, "after_xc")(part)
    by_y = exchange(part, "y")
    part = call(after_y_kernel, jax.ShapeDtypeStruct((NZ, 16, 128), F32), 1, "after_y")(by_y)
    by_z = exchange(part, "z")
    gram, change = call(
        functools.partial(final_kernel, points),
        (
            jax.ShapeDtypeStruct((4, 32), F32),
            jax.ShapeDtypeStruct((REAL * 8, 64), F32),
        ),
        2,
        "final",
        [pltpu.VMEM((SHAPES, 128), F32)],
    )(by_z, by_y.reshape(NY * 56, 128))
    return gram, change.reshape(REAL, 8, 64).transpose(0, 2, 1)


def solution(mesh):
    fine = Mesh(mesh.devices.reshape(NX, NY, NC, NZ), ("x", "y", "c", "z"))
    pts = ("x", "y", "c")
    rows = P((*pts, "z"), None)
    return jax.shard_map(
        on_device,
        mesh=fine,
        in_specs=(rows, rows, P(pts, "z", None), P()),
        out_specs=(P(pts, "z"), P(None, "z", pts)),
        check_vma=False,
    )
```

```python
import functools

import jax
import jax.numpy as jnp
from jax import lax
from jax.experimental import pallas as pl
from jax.experimental.pallas import tpu as pltpu
from jax.sharding import Mesh, PartitionSpec as P

F32 = jnp.float32
BF16 = jnp.bfloat16
VMEM = pl.BlockSpec(memory_space=pltpu.VMEM)

NX, NY, NC, NZ = 4, 8, 2, 8
BLADES, SHAPES, ORDER, REAL = 256, 64, 512, 24
CHUNKS = (2048, 2048, 2048)


def params(mib):
    return pltpu.CompilerParams(vmem_limit_bytes=mib * 1024 * 1024)


def pair(value):
    high = value.astype(BF16).astype(F32)
    return high, value - high


def halves(first, second):
    axis = first.ndim - 2
    row = lax.broadcasted_iota(jnp.int32, first.shape, axis)
    upper = jnp.where(row < 4, first, pltpu.roll(second, 4, axis))
    lower = jnp.where(row < 4, pltpu.roll(first, 4, axis), second)
    return upper, lower


def products_kernel(ids_hbm, dev_hbm, basis_hbm, sens_hbm, out_ref, ids_ref, dev_ref, basis_ref, sens_ref, gram_ref, turned_ref, picked_ref, sems):
    sens_copy = pltpu.make_async_copy(sens_hbm, sens_ref, sems.at[2 * len(CHUNKS)])
    ids_copy = pltpu.make_async_copy(ids_hbm, ids_ref, sems.at[2 * len(CHUNKS) + 1])
    copies = []
    for i, rows in enumerate(CHUNKS):
        span = pl.ds(sum(CHUNKS[:i]), rows)
        copies.append(pltpu.make_async_copy(dev_hbm.at[span, :], dev_ref.at[span, :], sems.at[2 * i]))
        copies.append(
            pltpu.make_async_copy(basis_hbm.at[:, span], basis_ref.at[:, span], sems.at[2 * i + 1])
        )
    sens_copy.start()
    for copy in copies:
        copy.start()
    ids_copy.start()

    sens_copy.wait()
    turned_ref[0:ORDER, :] = sens_ref[...].astype(F32).T
    even = turned_ref[pl.ds(0, ORDER // 2, 2), :]
    odd = turned_ref[pl.ds(1, ORDER // 2, 2), :]
    tiles = jnp.concatenate([even, odd], axis=1).reshape(16, 2, 8, 128)
    parts = halves(tiles[:, 0], tiles[:, 1])
    for x in range(NX):
        for c in range(NC):
            out_ref[2 * x + c, 160:192] = parts[c][4 * x : 4 * x + 4].reshape(32, 128).astype(BF16)

    gram = coef = None
    for i, rows in enumerate(CHUNKS):
        copies[2 * i].wait()
        copies[2 * i + 1].wait()
        start = sum(CHUNKS[:i])
        dev = dev_ref[start : start + rows, :]
        more = lax.dot_general(dev, dev, (((0,), (0,)), ((), ())), preferred_element_type=F32)
        gram = more if gram is None else gram + more
        more = jnp.dot(basis_ref[:, start : start + rows], dev, preferred_element_type=F32)
        coef = more if coef is None else coef + more
    gram_ref[...] = gram
    turned_ref[0:BLADES, :] = coef.T
    ids_copy.wait()

    parts = halves(gram[:, :128].reshape(32, 8, 128), gram[:, 128:].reshape(32, 8, 128))
    for x in range(NX):
        for c in range(NC):
            high, low = pair(parts[c][8 * x : 8 * x + 8].reshape(64, 128))
            out_ref[2 * x + c, 0:64] = high.astype(BF16)
            out_ref[2 * x + c, 64:128] = low.astype(BF16)

    lane = lax.broadcasted_iota(jnp.int32, (1, BLADES), 1)
    for r in range(REAL):
        blade = ids_ref[r]
        picked_ref[r : r + 1, 0:SHAPES] = turned_ref[pl.ds(blade, 1), :]
        row = jnp.where(lane == blade, gram_ref[pl.ds(blade, 1), :], 0.0)
        picked_ref[r : r + 1, 128:256] = row[:, :128] + row[:, 128:]
    coef = [picked_ref[8 * a : 8 * a + 8, 0:128] for a in range(3)]
    energy = [jnp.sum(picked_ref[8 * a : 8 * a + 8, 128:256], axis=1, keepdims=True) for a in range(3)]
    lane = lax.broadcasted_iota(jnp.int32, (8, 128), 1)
    upper = jnp.where(lane < 64, coef[0], pltpu.roll(coef[2], 64, 1))
    lower = jnp.where(lane < 64, coef[1], 0.0)
    for a in range(3):
        lower = jnp.where(lane == 64 + a, energy[a], lower)
    high, low = pair(jnp.concatenate([upper, lower], axis=0))
    for s in range(NX * NC):
        out_ref[s, 128:144] = high.astype(BF16)
        out_ref[s, 144:160] = low.astype(BF16)


def products(ids, dev, basis, sens):
    hbm = pl.BlockSpec(memory_space=pltpu.HBM)
    return pl.pallas_call(
        products_kernel,
        in_specs=[hbm] * 4,
        out_specs=VMEM,
        out_shape=jax.ShapeDtypeStruct((NX * NC, 192, 128), BF16),
        scratch_shapes=[
            pltpu.SMEM((REAL,), jnp.int32),
            pltpu.VMEM(dev.shape, dev.dtype),
            pltpu.VMEM(basis.shape, basis.dtype),
            pltpu.VMEM(sens.shape, sens.dtype),
            pltpu.VMEM((BLADES, BLADES), F32),
            pltpu.VMEM((ORDER, SHAPES), F32),
            pltpu.VMEM((REAL, 256), F32),
            pltpu.SemaphoreType.DMA((2 * len(CHUNKS) + 2,)),
        ],
        compiler_params=params(24),
        name="products",
    )(*(pltpu.with_memory_space_constraint(v, pltpu.HBM) for v in (ids, dev, basis, sens)))


def after_xc_kernel(in_ref, out_ref):
    gram = coef = 0.0
    for s in range(NX * NC):
        gram += in_ref[s, 0:64].astype(F32) + in_ref[s, 64:128].astype(F32)
        coef += in_ref[s, 128:144].astype(F32) + in_ref[s, 144:160].astype(F32)
    gram_high, gram_low = pair(gram)
    coef_high, coef_low = pair(coef)
    tiles = [in_ref[s, 160:192].astype(F32).reshape(4, 8, 128) for s in range(NX * NC)]
    parts = [halves(tiles[2 * a], tiles[2 * a + 1]) for a in range(NX)]
    for y in range(NY):
        rows = slice(8 * y, 8 * y + 8)
        out_ref[y, 0:16] = jnp.concatenate([gram_high[rows], gram_low[rows]], axis=0).astype(BF16)
        out_ref[y, 16:32] = coef_high.astype(BF16)
        out_ref[y, 32:48] = coef_low.astype(BF16)
        sens = [parts[a][y % 2][y // 2] for a in range(NX)]
        out_ref[y, 48:80] = jnp.concatenate(sens, axis=0).astype(BF16)


def after_y_kernel(in_ref, out_ref, sens_ref, rows_ref, block_ref):
    gram = coef = 0.0
    for y in range(NY):
        both = in_ref[y, 0:16].astype(F32)
        gram += both[0:8] + both[8:16]
        coef += in_ref[y, 16:32].astype(F32) + in_ref[y, 32:48].astype(F32)
        rows_ref[32 * y : 32 * y + 32, :] = in_ref[y, 48:80].astype(F32)
    row = lax.broadcasted_iota(jnp.int32, (8, 128), 0)
    lane = lax.broadcasted_iota(jnp.int32, (8, 128), 1)
    turned = pltpu.roll(gram, 4, 0)
    for z in range(NZ):
        block = gram if z < 4 else turned
        if z % 4 != 3:
            block = pltpu.roll(block, 96 - 32 * (z % 4), 1)
        out_ref[z, 0:8] = coef[0:8]
        out_ref[z, 8:16] = jnp.where((row < 4) & (lane >= 96), block, coef[8:16])
    for q in range(4):
        for s in range(NX * NC):
            first = 16 * (s // 2) + s % 2
            block_ref[q, pl.ds(first, NY, 2), :] = rows_ref[pl.ds(4 * s + q, NY, 32), :]
    sens_ref[...] = block_ref[...].astype(BF16)


def final_kernel(points, in_ref, sens_ref, gram_ref, change_ref):
    total = in_ref[0]
    for z in range(1, NZ):
        total += in_ref[z]
    upper, lower = total[0:8], total[8:16]
    gram_ref[...] = pltpu.roll(lower, 32, 1)[0:4, 0:32] / points
    coef = (upper, lower, pltpu.roll(upper, 64, 1))
    weights = []
    for a in range(3):
        energy = lower[:, 64 + a : 65 + a] / points
        weights.append(coef[a][:, 0:SHAPES] / jnp.sqrt(energy + 1e-05))
    high, rest = pair(jnp.concatenate(weights, axis=0))
    middle, low = pair(rest)
    terms = jnp.concatenate([high, middle, low], axis=0).astype(BF16)
    for q in range(4):
        block = jnp.dot(terms, sens_ref[q], preferred_element_type=F32)
        block = block[0:REAL] + (block[REAL : 2 * REAL] + block[2 * REAL :])
        change_ref[pl.ds(2 * q, REAL, 8), :] = block[:, 0:64]
        change_ref[pl.ds(2 * q + 1, REAL, 8), :] = block[:, 64:128]


def call(kernel, shape, count, name, scratch=()):
    return pl.pallas_call(
        kernel,
        in_specs=[VMEM] * count,
        out_specs=jax.tree.map(lambda _: VMEM, shape),
        out_shape=shape,
        scratch_shapes=scratch,
        compiler_params=params(8),
        name=name,
    )


def on_device(deviations, basis, sensitivity, blade_ids):
    points = float(deviations.shape[0] * NX * NY * NC * NZ)
    exchange = functools.partial(lax.all_to_all, split_axis=0, concat_axis=0, tiled=True)
    part = products(blade_ids, deviations, basis.T, sensitivity[0])
    part = exchange(part, ("x", "c"))
    part = call(after_xc_kernel, jax.ShapeDtypeStruct((NY, 80, 128), BF16), 1, "after_xc")(part)
    part = exchange(part, "y")
    part, sens = call(
        after_y_kernel,
        (
            jax.ShapeDtypeStruct((NZ, 16, 128), F32),
            jax.ShapeDtypeStruct((4, SHAPES, 128), BF16),
        ),
        1,
        "after_y",
        [pltpu.VMEM((NY * 32, 128), F32), pltpu.VMEM((4, SHAPES, 128), F32)],
    )(part)
    part = exchange(part, "z")
    gram, change = call(
        functools.partial(final_kernel, points),
        (
            jax.ShapeDtypeStruct((4, 32), F32),
            jax.ShapeDtypeStruct((REAL * 8, 64), F32),
        ),
        2,
        "final",
    )(part, sens)
    return gram, change.reshape(REAL, 8, 64).transpose(0, 2, 1)


def solution(mesh):
    fine = Mesh(mesh.devices.reshape(NX, NY, NC, NZ), ("x", "y", "c", "z"))
    pts = ("x", "y", "c")
    rows = P((*pts, "z"), None)
    return jax.shard_map(
        on_device,
        mesh=fine,
        in_specs=(rows, rows, P(pts, "z", None), P()),
        out_specs=(P(pts, "z"), P(None, "z", pts)),
        check_vma=False,
    )
```

```python
import functools

import jax
import jax.numpy as jnp
from jax import lax
from jax.experimental import pallas as pl
from jax.experimental.pallas import tpu as pltpu
from jax.sharding import Mesh, PartitionSpec as P

F32 = jnp.float32
BF16 = jnp.bfloat16
VMEM = pl.BlockSpec(memory_space=pltpu.VMEM)

NX, NY, NC, NZ = 4, 8, 2, 8
BLADES, SHAPES, ORDER, REAL = 256, 64, 512, 24
CHUNKS = (2048, 4096)


def params(mib):
    return pltpu.CompilerParams(vmem_limit_bytes=mib * 1024 * 1024)


def pair(value):
    high = value.astype(BF16).astype(F32)
    return high, value - high


def halves(first, second):
    axis = first.ndim - 2
    row = lax.broadcasted_iota(jnp.int32, first.shape, axis)
    upper = jnp.where(row < 4, first, pltpu.roll(second, 4, axis))
    lower = jnp.where(row < 4, pltpu.roll(first, 4, axis), second)
    return upper, lower


def products_kernel(ids_hbm, dev_hbm, basis_hbm, sens_hbm, out_ref, ids_ref, dev_ref, basis_ref, sens_ref, gram_ref, turned_ref, picked_ref, sems):
    sens_copy = pltpu.make_async_copy(sens_hbm, sens_ref, sems.at[2 * len(CHUNKS)])
    ids_copy = pltpu.make_async_copy(ids_hbm, ids_ref, sems.at[2 * len(CHUNKS) + 1])
    copies = []
    for i, rows in enumerate(CHUNKS):
        span = pl.ds(sum(CHUNKS[:i]), rows)
        copies.append(pltpu.make_async_copy(dev_hbm.at[span, :], dev_ref.at[span, :], sems.at[2 * i]))
        copies.append(
            pltpu.make_async_copy(basis_hbm.at[:, span], basis_ref.at[:, span], sems.at[2 * i + 1])
        )
    sens_copy.start()
    for copy in copies:
        copy.start()
    ids_copy.start()

    sens_copy.wait()
    turned_ref[0:ORDER, :] = sens_ref[...].astype(F32).T
    even = turned_ref[pl.ds(0, ORDER // 2, 2), :]
    odd = turned_ref[pl.ds(1, ORDER // 2, 2), :]
    tiles = jnp.concatenate([even, odd], axis=1).reshape(16, 2, 8, 128)
    parts = halves(tiles[:, 0], tiles[:, 1])
    for x in range(NX):
        for c in range(NC):
            out_ref[2 * x + c, 160:192] = parts[c][4 * x : 4 * x + 4].reshape(32, 128).astype(BF16)

    total = None
    for i, rows in enumerate(CHUNKS):
        copies[2 * i].wait()
        copies[2 * i + 1].wait()
        start = sum(CHUNKS[:i])
        dev = dev_ref[start : start + rows, :]
        left = jnp.concatenate([dev.T, basis_ref[:, start : start + rows]], axis=0)
        more = jnp.dot(left, dev, preferred_element_type=F32)
        total = more if total is None else total + more
    gram = total[0:BLADES]
    gram_ref[...] = gram
    turned_ref[0:BLADES, :] = total[BLADES:].T
    ids_copy.wait()

    parts = halves(gram[:, :128].reshape(32, 8, 128), gram[:, 128:].reshape(32, 8, 128))
    for x in range(NX):
        for c in range(NC):
            high, low = pair(parts[c][8 * x : 8 * x + 8].reshape(64, 128))
            out_ref[2 * x + c, 0:64] = high.astype(BF16)
            out_ref[2 * x + c, 64:128] = low.astype(BF16)

    lane = lax.broadcasted_iota(jnp.int32, (1, BLADES), 1)
    for r in range(REAL):
        blade = ids_ref[r]
        picked_ref[r : r + 1, 0:SHAPES] = turned_ref[pl.ds(blade, 1), :]
        row = jnp.where(lane == blade, gram_ref[pl.ds(blade, 1), :], 0.0)
        picked_ref[r : r + 1, 128:256] = row[:, :128] + row[:, 128:]
    coef = [picked_ref[8 * a : 8 * a + 8, 0:128] for a in range(3)]
    energy = [jnp.sum(picked_ref[8 * a : 8 * a + 8, 128:256], axis=1, keepdims=True) for a in range(3)]
    lane = lax.broadcasted_iota(jnp.int32, (8, 128), 1)
    upper = jnp.where(lane < 64, coef[0], pltpu.roll(coef[2], 64, 1))
    lower = jnp.where(lane < 64, coef[1], 0.0)
    for a in range(3):
        lower = jnp.where(lane == 64 + a, energy[a], lower)
    high, low = pair(jnp.concatenate([upper, lower], axis=0))
    for s in range(NX * NC):
        out_ref[s, 128:144] = high.astype(BF16)
        out_ref[s, 144:160] = low.astype(BF16)


def products(ids, dev, basis, sens):
    hbm = pl.BlockSpec(memory_space=pltpu.HBM)
    return pl.pallas_call(
        products_kernel,
        in_specs=[hbm] * 4,
        out_specs=VMEM,
        out_shape=jax.ShapeDtypeStruct((NX * NC, 192, 128), BF16),
        scratch_shapes=[
            pltpu.SMEM((REAL,), jnp.int32),
            pltpu.VMEM(dev.shape, dev.dtype),
            pltpu.VMEM(basis.shape, basis.dtype),
            pltpu.VMEM(sens.shape, sens.dtype),
            pltpu.VMEM((BLADES, BLADES), F32),
            pltpu.VMEM((ORDER, SHAPES), F32),
            pltpu.VMEM((REAL, 256), F32),
            pltpu.SemaphoreType.DMA((2 * len(CHUNKS) + 2,)),
        ],
        compiler_params=params(24),
        name="products",
    )(*(pltpu.with_memory_space_constraint(v, pltpu.HBM) for v in (ids, dev, basis, sens)))


def after_xc_kernel(in_ref, out_ref):
    gram = coef = 0.0
    for s in range(NX * NC):
        gram += in_ref[s, 0:64].astype(F32) + in_ref[s, 64:128].astype(F32)
        coef += in_ref[s, 128:144].astype(F32) + in_ref[s, 144:160].astype(F32)
    gram_high, gram_low = pair(gram)
    coef_high, coef_low = pair(coef)
    tiles = [in_ref[s, 160:192].astype(F32).reshape(4, 8, 128) for s in range(NX * NC)]
    parts = [halves(tiles[2 * a], tiles[2 * a + 1]) for a in range(NX)]
    for y in range(NY):
        rows = slice(8 * y, 8 * y + 8)
        out_ref[y, 0:16] = jnp.concatenate([gram_high[rows], gram_low[rows]], axis=0).astype(BF16)
        out_ref[y, 16:32] = coef_high.astype(BF16)
        out_ref[y, 32:48] = coef_low.astype(BF16)
        sens = [parts[a][y % 2][y // 2] for a in range(NX)]
        out_ref[y, 48:80] = jnp.concatenate(sens, axis=0).astype(BF16)


def after_y_kernel(in_ref, out_ref, sens_ref, rows_ref, block_ref):
    gram = coef = 0.0
    for y in range(NY):
        both = in_ref[y, 0:16].astype(F32)
        gram += both[0:8] + both[8:16]
        coef += in_ref[y, 16:32].astype(F32) + in_ref[y, 32:48].astype(F32)
        rows_ref[32 * y : 32 * y + 32, :] = in_ref[y, 48:80].astype(F32)
    row = lax.broadcasted_iota(jnp.int32, (8, 128), 0)
    lane = lax.broadcasted_iota(jnp.int32, (8, 128), 1)
    turned = pltpu.roll(gram, 4, 0)
    for z in range(NZ):
        block = gram if z < 4 else turned
        if z % 4 != 3:
            block = pltpu.roll(block, 96 - 32 * (z % 4), 1)
        out_ref[z, 0:8] = coef[0:8]
        out_ref[z, 8:16] = jnp.where((row < 4) & (lane >= 96), block, coef[8:16])
    for q in range(4):
        for s in range(NX * NC):
            first = 16 * (s // 2) + s % 2
            block_ref[q, pl.ds(first, NY, 2), :] = rows_ref[pl.ds(4 * s + q, NY, 32), :]
    sens_ref[...] = block_ref[...].astype(BF16)


def final_kernel(points, in_ref, sens_ref, gram_ref, change_ref):
    total = in_ref[0]
    for z in range(1, NZ):
        total += in_ref[z]
    upper, lower = total[0:8], total[8:16]
    gram_ref[...] = pltpu.roll(lower, 32, 1)[0:4, 0:32] / points
    coef = (upper, lower, pltpu.roll(upper, 64, 1))
    weights = []
    for a in range(3):
        energy = lower[:, 64 + a : 65 + a] / points
        weights.append(coef[a][:, 0:SHAPES] / jnp.sqrt(energy + 1e-05))
    high, rest = pair(jnp.concatenate(weights, axis=0))
    middle, low = pair(rest)
    terms = jnp.concatenate([high, middle, low], axis=0).astype(BF16)
    for q in range(4):
        block = jnp.dot(terms, sens_ref[q], preferred_element_type=F32)
        block = block[0:REAL] + (block[REAL : 2 * REAL] + block[2 * REAL :])
        change_ref[pl.ds(2 * q, REAL, 8), :] = block[:, 0:64]
        change_ref[pl.ds(2 * q + 1, REAL, 8), :] = block[:, 64:128]


def call(kernel, shape, count, name, scratch=()):
    return pl.pallas_call(
        kernel,
        in_specs=[VMEM] * count,
        out_specs=jax.tree.map(lambda _: VMEM, shape),
        out_shape=shape,
        scratch_shapes=scratch,
        compiler_params=params(8),
        name=name,
    )


def on_device(deviations, basis, sensitivity, blade_ids):
    points = float(deviations.shape[0] * NX * NY * NC * NZ)
    exchange = functools.partial(lax.all_to_all, split_axis=0, concat_axis=0, tiled=True)
    part = products(blade_ids, deviations, basis.T, sensitivity[0])
    part = exchange(part, ("x", "c"))
    part = call(after_xc_kernel, jax.ShapeDtypeStruct((NY, 80, 128), BF16), 1, "after_xc")(part)
    part = exchange(part, "y")
    part, sens = call(
        after_y_kernel,
        (
            jax.ShapeDtypeStruct((NZ, 16, 128), F32),
            jax.ShapeDtypeStruct((4, SHAPES, 128), BF16),
        ),
        1,
        "after_y",
        [pltpu.VMEM((NY * 32, 128), F32), pltpu.VMEM((4, SHAPES, 128), F32)],
    )(part)
    part = exchange(part, "z")
    gram, change = call(
        functools.partial(final_kernel, points),
        (
            jax.ShapeDtypeStruct((4, 32), F32),
            jax.ShapeDtypeStruct((REAL * 8, 64), F32),
        ),
        2,
        "final",
    )(part, sens)
    return gram, change.reshape(REAL, 8, 64).transpose(0, 2, 1)


def solution(mesh):
    fine = Mesh(mesh.devices.reshape(NX, NY, NC, NZ), ("x", "y", "c", "z"))
    pts = ("x", "y", "c")
    rows = P((*pts, "z"), None)
    return jax.shard_map(
        on_device,
        mesh=fine,
        in_specs=(rows, rows, P(pts, "z", None), P()),
        out_specs=(P(pts, "z"), P(None, "z", pts)),
        check_vma=False,
    )
```

```python
import functools

import jax
import jax.numpy as jnp
from jax import lax
from jax.experimental import pallas as pl
from jax.experimental.pallas import tpu as pltpu
from jax.sharding import Mesh, PartitionSpec as P

F32 = jnp.float32
BF16 = jnp.bfloat16
VMEM = pl.BlockSpec(memory_space=pltpu.VMEM)

NX, NY, NC, NZ = 4, 8, 2, 8
BLADES, SHAPES, ORDER, REAL = 256, 64, 512, 24
CHUNKS = (3072,) * 2


def params(mib):
    return pltpu.CompilerParams(vmem_limit_bytes=mib * 1024 * 1024)


def pair(value):
    high = value.astype(BF16).astype(F32)
    return high, value - high


def halves(first, second):
    axis = first.ndim - 2
    row = lax.broadcasted_iota(jnp.int32, first.shape, axis)
    upper = jnp.where(row < 4, first, pltpu.roll(second, 4, axis))
    lower = jnp.where(row < 4, pltpu.roll(first, 4, axis), second)
    return upper, lower


def products_kernel(ids_hbm, dev_hbm, basis_hbm, sens_hbm, out_ref, ids_ref, dev_ref, basis_ref, sens_ref, total_ref, turned_ref, picked_ref, sems):
    sens_copy = pltpu.make_async_copy(sens_hbm, sens_ref, sems.at[2 * len(CHUNKS)])
    ids_copy = pltpu.make_async_copy(ids_hbm, ids_ref, sems.at[2 * len(CHUNKS) + 1])
    copies = []
    for i, rows in enumerate(CHUNKS):
        span = pl.ds(sum(CHUNKS[:i]), rows)
        copies.append(pltpu.make_async_copy(dev_hbm.at[span, :], dev_ref.at[span, :], sems.at[2 * i]))
        copies.append(
            pltpu.make_async_copy(basis_hbm.at[:, span], basis_ref.at[:, span], sems.at[2 * i + 1])
        )
    sens_copy.start()
    for copy in copies:
        copy.start()
    ids_copy.start()

    total_ref[...] = jnp.zeros_like(total_ref)
    sens_copy.wait()
    turned_ref[0:ORDER, :] = sens_ref[...].astype(F32).T
    even = turned_ref[pl.ds(0, ORDER // 2, 2), :]
    odd = turned_ref[pl.ds(1, ORDER // 2, 2), :]
    tiles = jnp.concatenate([even, odd], axis=1).reshape(16, 2, 8, 128)
    parts = halves(tiles[:, 0], tiles[:, 1])
    for x in range(NX):
        for c in range(NC):
            out_ref[2 * x + c, 160:192] = parts[c][4 * x : 4 * x + 4].reshape(32, 128).astype(BF16)

    rows = CHUNKS[0]

    def step(i, carry):
        span = pl.ds(pl.multiple_of(i * rows, rows), rows)
        pltpu.make_async_copy(dev_hbm.at[span, :], dev_ref.at[span, :], sems.at[2 * i]).wait()
        pltpu.make_async_copy(basis_hbm.at[:, span], basis_ref.at[:, span], sems.at[2 * i + 1]).wait()
        dev = dev_ref[span, :]
        left = jnp.concatenate([dev.T, basis_ref[:, span]], axis=0)
        more = jnp.dot(left, dev, preferred_element_type=F32)
        total_ref[...] += more
        return carry

    lax.fori_loop(0, len(CHUNKS), step, 0)
    gram = total_ref[0:BLADES]
    turned_ref[0:BLADES, :] = total_ref[BLADES:, :].T
    ids_copy.wait()

    parts = halves(gram[:, :128].reshape(32, 8, 128), gram[:, 128:].reshape(32, 8, 128))
    for x in range(NX):
        for c in range(NC):
            high, low = pair(parts[c][8 * x : 8 * x + 8].reshape(64, 128))
            out_ref[2 * x + c, 0:64] = high.astype(BF16)
            out_ref[2 * x + c, 64:128] = low.astype(BF16)

    lane = lax.broadcasted_iota(jnp.int32, (1, BLADES), 1)
    for r in range(REAL):
        blade = ids_ref[r]
        picked_ref[r : r + 1, 0:SHAPES] = turned_ref[pl.ds(blade, 1), :]
        row = jnp.where(lane == blade, total_ref[pl.ds(blade, 1), :], 0.0)
        picked_ref[r : r + 1, 128:256] = row[:, :128] + row[:, 128:]
    coef = [picked_ref[8 * a : 8 * a + 8, 0:128] for a in range(3)]
    energy = [jnp.sum(picked_ref[8 * a : 8 * a + 8, 128:256], axis=1, keepdims=True) for a in range(3)]
    lane = lax.broadcasted_iota(jnp.int32, (8, 128), 1)
    upper = jnp.where(lane < 64, coef[0], pltpu.roll(coef[2], 64, 1))
    lower = jnp.where(lane < 64, coef[1], 0.0)
    for a in range(3):
        lower = jnp.where(lane == 64 + a, energy[a], lower)
    high, low = pair(jnp.concatenate([upper, lower], axis=0))
    for s in range(NX * NC):
        out_ref[s, 128:144] = high.astype(BF16)
        out_ref[s, 144:160] = low.astype(BF16)


def products(ids, dev, basis, sens):
    hbm = pl.BlockSpec(memory_space=pltpu.HBM)
    return pl.pallas_call(
        products_kernel,
        in_specs=[hbm] * 4,
        out_specs=VMEM,
        out_shape=jax.ShapeDtypeStruct((NX * NC, 192, 128), BF16),
        scratch_shapes=[
            pltpu.SMEM((REAL,), jnp.int32),
            pltpu.VMEM(dev.shape, dev.dtype),
            pltpu.VMEM(basis.shape, basis.dtype),
            pltpu.VMEM(sens.shape, sens.dtype),
            pltpu.VMEM((BLADES + SHAPES, BLADES), F32),
            pltpu.VMEM((ORDER, SHAPES), F32),
            pltpu.VMEM((REAL, 256), F32),
            pltpu.SemaphoreType.DMA((2 * len(CHUNKS) + 2,)),
        ],
        compiler_params=params(24),
        name="products",
    )(*(pltpu.with_memory_space_constraint(v, pltpu.HBM) for v in (ids, dev, basis, sens)))


def after_xc_kernel(in_ref, out_ref):
    gram = coef = 0.0
    for s in range(NX * NC):
        gram += in_ref[s, 0:64].astype(F32) + in_ref[s, 64:128].astype(F32)
        coef += in_ref[s, 128:144].astype(F32) + in_ref[s, 144:160].astype(F32)
    gram_high, gram_low = pair(gram)
    coef_high, coef_low = pair(coef)
    tiles = [in_ref[s, 160:192].astype(F32).reshape(4, 8, 128) for s in range(NX * NC)]
    parts = [halves(tiles[2 * a], tiles[2 * a + 1]) for a in range(NX)]
    for y in range(NY):
        rows = slice(8 * y, 8 * y + 8)
        out_ref[y, 0:16] = jnp.concatenate([gram_high[rows], gram_low[rows]], axis=0).astype(BF16)
        out_ref[y, 16:32] = coef_high.astype(BF16)
        out_ref[y, 32:48] = coef_low.astype(BF16)
        sens = [parts[a][y % 2][y // 2] for a in range(NX)]
        out_ref[y, 48:80] = jnp.concatenate(sens, axis=0).astype(BF16)


def after_y_kernel(in_ref, out_ref, sens_ref, rows_ref, block_ref):
    gram = coef = 0.0
    for y in range(NY):
        both = in_ref[y, 0:16].astype(F32)
        gram += both[0:8] + both[8:16]
        coef += in_ref[y, 16:32].astype(F32) + in_ref[y, 32:48].astype(F32)
        rows_ref[32 * y : 32 * y + 32, :] = in_ref[y, 48:80].astype(F32)
    row = lax.broadcasted_iota(jnp.int32, (8, 128), 0)
    lane = lax.broadcasted_iota(jnp.int32, (8, 128), 1)
    turned = pltpu.roll(gram, 4, 0)
    for z in range(NZ):
        block = gram if z < 4 else turned
        if z % 4 != 3:
            block = pltpu.roll(block, 96 - 32 * (z % 4), 1)
        out_ref[z, 0:8] = coef[0:8]
        out_ref[z, 8:16] = jnp.where((row < 4) & (lane >= 96), block, coef[8:16])
    for q in range(4):
        for s in range(NX * NC):
            first = 16 * (s // 2) + s % 2
            block_ref[q, pl.ds(first, NY, 2), :] = rows_ref[pl.ds(4 * s + q, NY, 32), :]
    sens_ref[...] = block_ref[...].astype(BF16)


def final_kernel(points, in_ref, sens_ref, gram_ref, change_ref):
    total = in_ref[0]
    for z in range(1, NZ):
        total += in_ref[z]
    upper, lower = total[0:8], total[8:16]
    gram_ref[...] = pltpu.roll(lower, 32, 1)[0:4, 0:32] / points
    coef = (upper, lower, pltpu.roll(upper, 64, 1))
    weights = []
    for a in range(3):
        energy = lower[:, 64 + a : 65 + a] / points
        weights.append(coef[a][:, 0:SHAPES] / jnp.sqrt(energy + 1e-05))
    high, rest = pair(jnp.concatenate(weights, axis=0))
    middle, low = pair(rest)
    terms = jnp.concatenate([high, middle, low], axis=0).astype(BF16)
    for q in range(4):
        block = jnp.dot(terms, sens_ref[q], preferred_element_type=F32)
        block = block[0:REAL] + (block[REAL : 2 * REAL] + block[2 * REAL :])
        change_ref[pl.ds(2 * q, REAL, 8), :] = block[:, 0:64]
        change_ref[pl.ds(2 * q + 1, REAL, 8), :] = block[:, 64:128]


def call(kernel, shape, count, name, scratch=()):
    return pl.pallas_call(
        kernel,
        in_specs=[VMEM] * count,
        out_specs=jax.tree.map(lambda _: VMEM, shape),
        out_shape=shape,
        scratch_shapes=scratch,
        compiler_params=params(8),
        name=name,
    )


def on_device(deviations, basis, sensitivity, blade_ids):
    points = float(deviations.shape[0] * NX * NY * NC * NZ)
    exchange = functools.partial(lax.all_to_all, split_axis=0, concat_axis=0, tiled=True)
    part = products(blade_ids, deviations, basis.T, sensitivity[0])
    part = exchange(part, ("x", "c"))
    part = call(after_xc_kernel, jax.ShapeDtypeStruct((NY, 80, 128), BF16), 1, "after_xc")(part)
    part = exchange(part, "y")
    part, sens = call(
        after_y_kernel,
        (
            jax.ShapeDtypeStruct((NZ, 16, 128), F32),
            jax.ShapeDtypeStruct((4, SHAPES, 128), BF16),
        ),
        1,
        "after_y",
        [pltpu.VMEM((NY * 32, 128), F32), pltpu.VMEM((4, SHAPES, 128), F32)],
    )(part)
    part = exchange(part, "z")
    gram, change = call(
        functools.partial(final_kernel, points),
        (
            jax.ShapeDtypeStruct((4, 32), F32),
            jax.ShapeDtypeStruct((REAL * 8, 64), F32),
        ),
        2,
        "final",
    )(part, sens)
    return gram, change.reshape(REAL, 8, 64).transpose(0, 2, 1)


def solution(mesh):
    fine = Mesh(mesh.devices.reshape(NX, NY, NC, NZ), ("x", "y", "c", "z"))
    pts = ("x", "y", "c")
    rows = P((*pts, "z"), None)
    return jax.shard_map(
        on_device,
        mesh=fine,
        in_specs=(rows, rows, P(pts, "z", None), P()),
        out_specs=(P(pts, "z"), P(None, "z", pts)),
        check_vma=False,
    )
```

```python
import functools

import jax
import jax.numpy as jnp
from jax import lax
from jax.experimental import pallas as pl
from jax.experimental.pallas import tpu as pltpu
from jax.sharding import Mesh, PartitionSpec as P

F32 = jnp.float32
BF16 = jnp.bfloat16
VMEM = pl.BlockSpec(memory_space=pltpu.VMEM)

NX, NY, NC, NZ = 4, 8, 2, 8
BLADES, SHAPES, ORDER, REAL = 256, 64, 512, 24
CHUNKS = (3072,) * 2


def params(mib):
    return pltpu.CompilerParams(vmem_limit_bytes=mib * 1024 * 1024)


def pair(value):
    high = value.astype(BF16).astype(F32)
    return high, value - high


def halves(first, second):
    axis = first.ndim - 2
    row = lax.broadcasted_iota(jnp.int32, first.shape, axis)
    upper = jnp.where(row < 4, first, pltpu.roll(second, 4, axis))
    lower = jnp.where(row < 4, pltpu.roll(first, 4, axis), second)
    return upper, lower


def products_kernel(ids_hbm, dev_hbm, basis_hbm, sens_hbm, out_ref, ids_ref, dev_ref, basis_ref, sens_ref, total_ref, turned_ref, picked_ref, sems):
    sens_copy = pltpu.make_async_copy(sens_hbm, sens_ref, sems.at[2 * len(CHUNKS)])
    ids_copy = pltpu.make_async_copy(ids_hbm, ids_ref, sems.at[2 * len(CHUNKS) + 1])
    copies = []
    for i, rows in enumerate(CHUNKS):
        span = pl.ds(sum(CHUNKS[:i]), rows)
        copies.append(pltpu.make_async_copy(dev_hbm.at[span, :], dev_ref.at[span, :], sems.at[2 * i]))
        copies.append(
            pltpu.make_async_copy(basis_hbm.at[:, span], basis_ref.at[:, span], sems.at[2 * i + 1])
        )
    sens_copy.start()
    for copy in copies[1::2] + copies[::2]:
        copy.start()
    ids_copy.start()

    total_ref[...] = jnp.zeros_like(total_ref)
    sens_copy.wait()
    turned_ref[0:ORDER, :] = sens_ref[...].astype(F32).T
    even = turned_ref[pl.ds(0, ORDER // 2, 2), :]
    odd = turned_ref[pl.ds(1, ORDER // 2, 2), :]
    tiles = jnp.concatenate([even, odd], axis=1).reshape(16, 2, 8, 128)
    parts = halves(tiles[:, 0], tiles[:, 1])
    for x in range(NX):
        for c in range(NC):
            out_ref[2 * x + c, 160:192] = parts[c][4 * x : 4 * x + 4].reshape(32, 128).astype(BF16)

    rows = CHUNKS[0]

    def step(i, carry):
        span = pl.ds(pl.multiple_of(i * rows, rows), rows)
        pltpu.make_async_copy(dev_hbm.at[span, :], dev_ref.at[span, :], sems.at[2 * i]).wait()
        pltpu.make_async_copy(basis_hbm.at[:, span], basis_ref.at[:, span], sems.at[2 * i + 1]).wait()
        dev = dev_ref[span, :]
        left = jnp.concatenate([dev.T, basis_ref[:, span]], axis=0)
        more = jnp.dot(left, dev, preferred_element_type=F32)
        total_ref[...] += more
        return carry

    lax.fori_loop(0, len(CHUNKS), step, 0)
    gram = total_ref[0:BLADES]
    turned_ref[0:BLADES, :] = total_ref[BLADES:, :].T
    ids_copy.wait()

    parts = halves(gram[:, :128].reshape(32, 8, 128), gram[:, 128:].reshape(32, 8, 128))
    for x in range(NX):
        for c in range(NC):
            high, low = pair(parts[c][8 * x : 8 * x + 8].reshape(64, 128))
            out_ref[2 * x + c, 0:64] = high.astype(BF16)
            out_ref[2 * x + c, 64:128] = low.astype(BF16)

    lane = lax.broadcasted_iota(jnp.int32, (1, BLADES), 1)
    for r in range(REAL):
        blade = ids_ref[r]
        picked_ref[r : r + 1, 0:SHAPES] = turned_ref[pl.ds(blade, 1), :]
        row = jnp.where(lane == blade, total_ref[pl.ds(blade, 1), :], 0.0)
        picked_ref[r : r + 1, 128:256] = row[:, :128] + row[:, 128:]
    coef = [picked_ref[8 * a : 8 * a + 8, 0:128] for a in range(3)]
    energy = [jnp.sum(picked_ref[8 * a : 8 * a + 8, 128:256], axis=1, keepdims=True) for a in range(3)]
    lane = lax.broadcasted_iota(jnp.int32, (8, 128), 1)
    upper = jnp.where(lane < 64, coef[0], pltpu.roll(coef[2], 64, 1))
    lower = jnp.where(lane < 64, coef[1], 0.0)
    for a in range(3):
        lower = jnp.where(lane == 64 + a, energy[a], lower)
    high, low = pair(jnp.concatenate([upper, lower], axis=0))
    for s in range(NX * NC):
        out_ref[s, 128:144] = high.astype(BF16)
        out_ref[s, 144:160] = low.astype(BF16)


def products(ids, dev, basis, sens):
    hbm = pl.BlockSpec(memory_space=pltpu.HBM)
    return pl.pallas_call(
        products_kernel,
        in_specs=[hbm] * 4,
        out_specs=VMEM,
        out_shape=jax.ShapeDtypeStruct((NX * NC, 192, 128), BF16),
        scratch_shapes=[
            pltpu.SMEM((REAL,), jnp.int32),
            pltpu.VMEM(dev.shape, dev.dtype),
            pltpu.VMEM(basis.shape, basis.dtype),
            pltpu.VMEM(sens.shape, sens.dtype),
            pltpu.VMEM((BLADES + SHAPES, BLADES), F32),
            pltpu.VMEM((ORDER, SHAPES), F32),
            pltpu.VMEM((REAL, 256), F32),
            pltpu.SemaphoreType.DMA((2 * len(CHUNKS) + 2,)),
        ],
        compiler_params=params(24),
        name="products",
    )(*(pltpu.with_memory_space_constraint(v, pltpu.HBM) for v in (ids, dev, basis, sens)))


def after_xc_kernel(in_ref, out_ref):
    gram = coef = 0.0
    for s in range(NX * NC):
        gram += in_ref[s, 0:64].astype(F32) + in_ref[s, 64:128].astype(F32)
        coef += in_ref[s, 128:144].astype(F32) + in_ref[s, 144:160].astype(F32)
    gram_high, gram_low = pair(gram)
    coef_high, coef_low = pair(coef)
    tiles = [in_ref[s, 160:192].astype(F32).reshape(4, 8, 128) for s in range(NX * NC)]
    parts = [halves(tiles[2 * a], tiles[2 * a + 1]) for a in range(NX)]
    for y in range(NY):
        rows = slice(8 * y, 8 * y + 8)
        out_ref[y, 0:16] = jnp.concatenate([gram_high[rows], gram_low[rows]], axis=0).astype(BF16)
        out_ref[y, 16:32] = coef_high.astype(BF16)
        out_ref[y, 32:48] = coef_low.astype(BF16)
        sens = [parts[a][y % 2][y // 2] for a in range(NX)]
        out_ref[y, 48:80] = jnp.concatenate(sens, axis=0).astype(BF16)


def after_y_kernel(in_ref, out_ref, sens_ref, rows_ref, block_ref):
    gram = coef = 0.0
    for y in range(NY):
        both = in_ref[y, 0:16].astype(F32)
        gram += both[0:8] + both[8:16]
        coef += in_ref[y, 16:32].astype(F32) + in_ref[y, 32:48].astype(F32)
        rows_ref[32 * y : 32 * y + 32, :] = in_ref[y, 48:80].astype(F32)
    row = lax.broadcasted_iota(jnp.int32, (8, 128), 0)
    lane = lax.broadcasted_iota(jnp.int32, (8, 128), 1)
    turned = pltpu.roll(gram, 4, 0)
    for z in range(NZ):
        block = gram if z < 4 else turned
        if z % 4 != 3:
            block = pltpu.roll(block, 96 - 32 * (z % 4), 1)
        out_ref[z, 0:8] = coef[0:8]
        out_ref[z, 8:16] = jnp.where((row < 4) & (lane >= 96), block, coef[8:16])
    for q in range(4):
        for s in range(NX * NC):
            first = 16 * (s // 2) + s % 2
            block_ref[q, pl.ds(first, NY, 2), :] = rows_ref[pl.ds(4 * s + q, NY, 32), :]
    sens_ref[...] = block_ref[...].astype(BF16)


def final_kernel(points, in_ref, sens_ref, gram_ref, change_ref):
    total = in_ref[0]
    for z in range(1, NZ):
        total += in_ref[z]
    upper, lower = total[0:8], total[8:16]
    gram_ref[...] = pltpu.roll(lower, 32, 1)[0:4, 0:32] / points
    coef = (upper, lower, pltpu.roll(upper, 64, 1))
    weights = []
    for a in range(3):
        energy = lower[:, 64 + a : 65 + a] / points
        weights.append(coef[a][:, 0:SHAPES] / jnp.sqrt(energy + 1e-05))
    high, rest = pair(jnp.concatenate(weights, axis=0))
    middle, low = pair(rest)
    terms = jnp.concatenate([high, middle, low], axis=0).astype(BF16)
    for q in range(4):
        block = jnp.dot(terms, sens_ref[q], preferred_element_type=F32)
        block = block[0:REAL] + (block[REAL : 2 * REAL] + block[2 * REAL :])
        change_ref[pl.ds(2 * q, REAL, 8), :] = block[:, 0:64]
        change_ref[pl.ds(2 * q + 1, REAL, 8), :] = block[:, 64:128]


def call(kernel, shape, count, name, scratch=()):
    return pl.pallas_call(
        kernel,
        in_specs=[VMEM] * count,
        out_specs=jax.tree.map(lambda _: VMEM, shape),
        out_shape=shape,
        scratch_shapes=scratch,
        compiler_params=params(8),
        name=name,
    )


def on_device(deviations, basis, sensitivity, blade_ids):
    points = float(deviations.shape[0] * NX * NY * NC * NZ)
    exchange = functools.partial(lax.all_to_all, split_axis=0, concat_axis=0, tiled=True)
    part = products(blade_ids, deviations, basis.T, sensitivity[0])
    part = exchange(part, ("x", "c"))
    part = call(after_xc_kernel, jax.ShapeDtypeStruct((NY, 80, 128), BF16), 1, "after_xc")(part)
    part = exchange(part, "y")
    part, sens = call(
        after_y_kernel,
        (
            jax.ShapeDtypeStruct((NZ, 16, 128), F32),
            jax.ShapeDtypeStruct((4, SHAPES, 128), BF16),
        ),
        1,
        "after_y",
        [pltpu.VMEM((NY * 32, 128), F32), pltpu.VMEM((4, SHAPES, 128), F32)],
    )(part)
    part = exchange(part, "z")
    gram, change = call(
        functools.partial(final_kernel, points),
        (
            jax.ShapeDtypeStruct((4, 32), F32),
            jax.ShapeDtypeStruct((REAL * 8, 64), F32),
        ),
        2,
        "final",
    )(part, sens)
    return gram, change.reshape(REAL, 8, 64).transpose(0, 2, 1)


def solution(mesh):
    fine = Mesh(mesh.devices.reshape(NX, NY, NC, NZ), ("x", "y", "c", "z"))
    pts = ("x", "y", "c")
    rows = P((*pts, "z"), None)
    return jax.shard_map(
        on_device,
        mesh=fine,
        in_specs=(rows, rows, P(pts, "z", None), P()),
        out_specs=(P(pts, "z"), P(None, "z", pts)),
        check_vma=False,
    )
```
